128 devices in a mesh: row: 8 (over y, z_lo), col: 16 (over x, z_hi, core).
Axes of the slice: x: 4, y: 4, z: 4 (z_hi: 2, z_lo: 2; z = z_hi * 2 + z_lo), core: 2. Of those that a mesh axis runs over, the one named last changes fastest.
Arguments:
- eigvecs: float32 [512, 65536], P(('col', 'row')), may hold values from -6 to 6
- row_map: int32 [65536], replicated, may hold values from 0 to 65535, as said below
- reflectors: float32 [16, 512, 65536], P(None, 'col', 'row'), may hold values from -0.0234375 to 0.0234375
- panel_factor: float32 [2, 512, 512], replicated, may hold values from -4 to 4
- owners: int32 [16], replicated, may hold values from 0 to 15, each once
Outputs:
- back_vectors: float32 [512, 65536], P('col', 'row')
The draws below stay inside these ranges and needn't reach their ends.
Inputs may be any that keep to these rules, and one draw needn't show every extreme that they name: row_map is a permutation of 0 to 65535 that moves aligned blocks of 64 rows whole, keeping the order inside a block. owners is a permutation; only its first 2 entries are read, so only those slots of reflectors are used.
All inputs are finite; a program needn't handle non-finite values.
Results may differ from the reference program's by a relative error of at most 0.0001.
Values sent between devices are 32-bit elements; how exact they have to be, the bound alone decides.
A program may use at most 128 MiB of HBM per device.

```python
import jax
import jax.numpy as jnp
from jax import lax

N = 65536
PW = 512
PANELS = 2
NB = 64
K = 512
SLOTS = 16


def draw_row_map(key, part):
    blocks = N // NB
    order = jax.random.permutation(key, blocks).astype(jnp.int32)
    place = jnp.arange(N, dtype=jnp.int32)
    return (order[place // NB] * NB + place % NB).astype(jnp.int32)


def steps_of(stream_key, extent, shards, low, top_value):
    gain, own = 1.0, jax.random.fold_in(stream_key, 6)
    for dim, shards_of in shards:
        steps = jnp.exp(jax.random.uniform(jax.random.fold_in(own, dim), (shards_of,), jnp.float32, low / len(shards), top_value / len(shards)))
        gain = gain * jnp.repeat(steps, extent[dim] // shards_of).reshape([-1 if axis == dim else 1 for axis in range(len(extent))])
    return gain


def gaussian(own_key, shape, width, reach, cuts=(), kind=jnp.bfloat16):
    gain = steps_of(own_key, shape, cuts, -0.22, 0.18) if cuts else 1.0
    result = jax.random.normal(own_key, shape, jnp.float32) * width * gain
    return jnp.minimum(jnp.maximum(result, -reach), reach).astype(kind)


def setup_inputs(seed: int = 0) -> dict:
    keys = jax.random.split(jax.random.key(seed), 6)
    eigvecs = gaussian(keys[0], (K, N), 1.0, 6.0, ((0, 128),), jnp.float32)
    row_map = draw_row_map(jax.random.fold_in(keys[5], 71), 0)
    reflectors = gaussian(keys[2], (SLOTS, PW, N), N ** -0.5, 0.0234375, ((1, 16), (2, 8)), jnp.float32)
    panel_factor = gaussian(keys[3], (PANELS, PW, PW), (max(1, PW * PW // (2 * N))) ** -0.5, 4.0, (), jnp.float32)
    owners = jax.random.permutation(keys[4], SLOTS).astype(jnp.int32)
    return {"eigvecs": eigvecs, "row_map": row_map, "reflectors": reflectors, "panel_factor": panel_factor, "owners": owners}


def reference(eigvecs, row_map, reflectors, panel_factor, owners):
    current = jnp.take(eigvecs, row_map, axis=1)
    for panel in range(PANELS):
        vectors = reflectors[owners[panel]]
        factor = jnp.triu(panel_factor[panel])
        project = jnp.dot(current, vectors.T, precision=lax.Precision.HIGHEST, preferred_element_type=jnp.float32)
        scaled = jnp.dot(project, factor.T, precision=lax.Precision.HIGHEST, preferred_element_type=jnp.float32)
        current = current - jnp.dot(scaled, vectors, precision=lax.Precision.HIGHEST, preferred_element_type=jnp.float32)
    return current
```

```python
import jax
import jax.numpy as jnp
from jax import lax
from jax.sharding import PartitionSpec as P

PANELS = 2
NB = 64


def hdot(left, right):
    return jnp.dot(left, right, precision=lax.Precision.HIGHEST, preferred_element_type=jnp.float32)


def per_device(eigvecs, row_map, reflectors, panel_factor, owners):
    rows, cols = lax.axis_size("row"), lax.axis_size("col")
    eig_local, total_rows = eigvecs.shape
    piece = total_rows // (rows * cols)
    block_count = total_rows // NB
    block_index = row_map.reshape(block_count, NB)[:, 0] // NB
    block_index = block_index.reshape(rows, cols, piece // NB).transpose(1, 0, 2).reshape(block_count)
    blocked = eigvecs.reshape(eig_local, block_count, NB)
    ordered = jnp.take(blocked, block_index, axis=1).reshape(eig_local, rows * cols, piece)
    arrived = lax.all_to_all(ordered, ("col", "row"), split_axis=1, concat_axis=0, tiled=True)
    current = arrived.reshape(eig_local * rows * cols, piece)
    for panel in range(PANELS):
        mine = reflectors[owners[panel]]
        mine = mine.reshape(mine.shape[0], cols, piece)
        vectors = lax.all_to_all(mine, "col", split_axis=1, concat_axis=0, tiled=True)
        vectors = vectors.reshape(-1, piece)
        upper = jnp.triu(panel_factor[panel])
        project = lax.psum(hdot(current, vectors.T), ("row", "col"))
        scaled = hdot(project, upper.T)
        current = current - hdot(scaled, vectors)
    out = lax.all_to_all(current.reshape(cols, -1, piece), "col", split_axis=0, concat_axis=0, tiled=True)
    return out.transpose(1, 0, 2).reshape(-1, cols * piece)


def solution(mesh):
    placed = (P(("col", "row"), None), P(), P(None, "col", "row"), P(), P())
    return jax.shard_map(
        per_device, mesh=mesh, in_specs=placed, out_specs=P("col", "row"), check_vma=False
    )
```

```python
import functools

import jax
import jax.numpy as jnp
from jax import lax
from jax.experimental import pallas as pl
from jax.experimental.pallas import tpu as pltpu
from jax.sharding import PartitionSpec as P

PANELS = 2
NB = 64
MESH = pl.DeviceIdType.MESH
PLANE = [(dx, dh, dl) for dx in range(4) for dh in range(2) for dl in range(2)]
PEERS = PLANE[1:]
SLAB = [(dx, dh) for dx in range(4) for dh in range(2)]


def split(value):
    high = value.astype(jnp.bfloat16)
    return high, (value - high.astype(jnp.float32)).astype(jnp.bfloat16)


def product(left, right, contract):
    dims = (((1,), (contract,)), ((), ()))
    lh, ll = left
    rh, rl = right
    dot = functools.partial(lax.dot_general, dimension_numbers=dims, preferred_element_type=jnp.float32)
    return dot(lh, rh) + (dot(lh, rl) + dot(ll, rh))


def kernel(
    tiles, odd, eig, vin, factor, out,
    zg, za, zr, zf, vr, vh, vl, wp, wr, ws, wy, ys, yr,
    own_sem, va_s, va_r, vb_s, vb_r, za_s, za_r, zb_s, zb_r, zc_s, zc_r,
    ws_s, ws_r, wy_s, wy_r, ya_s, ya_r, zo_s, zo_r,
):
    row, col = lax.axis_index("row"), lax.axis_index("col")
    y, zl = lax.div(row, 2), lax.rem(row, 2)
    x, zh, core = lax.div(col, 4), lax.rem(lax.div(col, 2), 2), lax.rem(col, 2)

    def device(dx, dy, dh, dl, dc=0):
        there = (
            lax.rem(y + dy, 4) * 2 + lax.rem(zl + dl, 2),
            lax.rem(x + dx, 4) * 4 + lax.rem(zh + dh, 2) * 2 + lax.rem(core + dc, 2),
        )
        return there

    def remote(src, dst, send, recv, there):
        return pltpu.make_async_remote_copy(
            src_ref=src, dst_ref=dst, send_sem=send, recv_sem=recv, device_id=there, device_id_type=MESH
        )

    def plane_of(dx, dh, dl):
        return lax.rem(x + dx, 4) * 4 + lax.rem(zh + dh, 2) * 2 + lax.rem(zl + dl, 2)

    def slab_of(dx, dh):
        return lax.rem(x + dx, 4) * 2 + lax.rem(zh + dh, 2)

    here, mine = plane_of(0, 0, 0), slab_of(0, 0)
    piece = zf.shape[1]

    barrier = pltpu.get_barrier_semaphore()
    for dx, dh, dl in PEERS:
        pl.semaphore_signal(barrier, inc=1, device_id=device(dx, 0, dh, dl), device_id_type=MESH)
    for dy in (1, 2, 3):
        pl.semaphore_signal(barrier, inc=1, device_id=device(0, dy, 0, 0), device_id_type=MESH)
    pl.semaphore_signal(barrier, inc=1, device_id=device(0, 0, 0, 0, 1), device_id_type=MESH)
    pl.semaphore_wait(barrier, len(PEERS) + 4)

    def vector_sends(panel):
        copies = []
        for o, (dx, dh) in enumerate(SLAB):
            there = slab_of(dx, dh)
            src = vin.at[panel, :, pl.ds(pl.multiple_of(there * piece, piece), piece)]
            if o == 0:
                copies.append(pltpu.make_async_copy(src, vr.at[panel, col], own_sem.at[panel]))
            else:
                copies.append(
                    remote(src, vr.at[panel, col], va_s.at[panel, o], va_r.at[panel, o], device(dx, 0, dh, 0))
                )
        return copies

    def start(copies):
        for copy in copies:
            copy.start()
        return copies

    vectors_out = [start(vector_sends(0))]

    lane = lax.broadcasted_iota(jnp.int32, (4, 128), 1)

    def gather(dy, target):
        yy = lax.rem(y + dy, 4)

        def body(step, carry):
            xz, low = lax.div(step, 2), lax.rem(step, 2)
            first = (yy * 2 + low) * (8 * piece // NB) + xz * (piece // NB)
            for tile in range(piece // 128):
                one, two = first + 2 * tile, first + 2 * tile + 1
                a, b = eig[tiles[one]], eig[tiles[two]]
                a = jnp.where(jnp.full((4, 128), odd[one]) == 0, a, pltpu.roll(a, 64, 1))
                b = jnp.where(jnp.full((4, 128), odd[two]) == 1, b, pltpu.roll(b, 64, 1))
                target[step, :, tile * 128 : (tile + 1) * 128] = jnp.where(lane < 64, a, b)
            return carry

        lax.fori_loop(0, 16, body, 0)

    along_y = []
    for dy in (2, 1, 3):
        gather(dy, zg.at[dy])
        along_y.append(remote(zg.at[dy], za.at[dy], za_s.at[dy], za_r.at[dy], device(0, dy, 0, 0)))
        along_y[-1].start()
    gather(0, za.at[0])
    near = [
        remote(za.at[0, plane_of(*o)], zr.at[here, 0], zb_s.at[i], zb_r.at[i], device(o[0], 0, o[1], o[2]))
        for i, o in enumerate(PEERS)
    ]
    start(near)
    for copy in along_y:
        copy.wait()
    far = [
        remote(
            za.at[pl.ds(1, 3), plane_of(*o)], zr.at[here, pl.ds(1, 3)], zc_s.at[i], zc_r.at[i],
            device(o[0], 0, o[1], o[2]),
        )
        for i, o in enumerate(PEERS)
    ]
    start(far)
    own = pltpu.make_async_copy(za.at[:, here], zr.at[here], own_sem.at[2])
    own.start()
    vectors_out.append(start(vector_sends(1)))

    def exchange(panel):
        copies = []
        for o, (dx, dh) in enumerate(SLAB):
            source = lax.rem(x + 4 - dx, 4) * 4 + lax.rem(zh + dh, 2) * 2 + core
            if o == 0:
                vectors_out[panel][0].wait()
            else:
                vectors_out[panel][o].wait_recv()
            copies.append(
                remote(
                    vr.at[panel, source], vr.at[panel, source], vb_s.at[panel, o], vb_r.at[panel, o],
                    device(0, 0, 0, 0, 1),
                )
            )
            copies[-1].start()
        return copies

    def split_vectors(panel, copies):
        for copy in copies:
            copy.wait()

        def body(step, carry):
            high, low = split(vr[panel, step])
            vh[panel, pl.ds(pl.multiple_of(step * 32, 32), 32), :] = high
            vl[panel, pl.ds(pl.multiple_of(step * 32, 32), 32), :] = low
            return carry

        lax.fori_loop(0, 16, body, 0)

    split_vectors(0, exchange(0))
    for copy in near + far + [own]:
        copy.wait()

    def assemble(step, carry):
        chip, dy = lax.div(step, 4), lax.rem(step, 4)
        rows = jnp.concatenate([zr[2 * chip, dy], zr[2 * chip + 1, dy]], axis=0)
        place = chip * 32 + lax.rem(y + 4 - dy, 4) * 8
        zf[pl.ds(pl.multiple_of(place, 8), 8), :] = rows
        return carry

    lax.fori_loop(0, 32, assemble, 0)

    pending = []
    for panel in range(PANELS):
        if panel == 1:
            split_vectors(1, exchange(1))
        wp[panel] = product(split(zf[...]), (vh[panel], vl[panel]), 1).reshape(wp.shape[1:])
        spread = start([
            remote(
                wp.at[panel, plane_of(*o)], wr.at[panel, here], ws_s.at[panel, i], ws_r.at[panel, i],
                device(o[0], 0, o[1], o[2]),
            )
            for i, o in enumerate(PEERS)
        ])
        row_i = lax.broadcasted_iota(jnp.int32, factor.shape[1:], 0)
        col_i = lax.broadcasted_iota(jnp.int32, factor.shape[1:], 1)
        upper = split(jnp.where(row_i <= col_i, factor[panel], 0.0))
        total = wp[panel, here]
        for (dx, dh, dl), copy in zip(PEERS, spread):
            copy.wait_recv()
            total = total + wr[panel, lax.rem(x + 4 - dx, 4) * 4 + lax.rem(zh + dh, 2) * 2 + lax.rem(zl + dl, 2)]
        ws[panel] = total
        across = start([
            remote(ws.at[panel], wy.at[panel, dy], wy_s.at[panel, dy], wy_r.at[panel, dy], device(0, dy, 0, 0))
            for dy in (1, 2, 3)
        ])
        for dy, copy in zip((1, 2, 3), across):
            copy.wait_recv()
            total = total + wy[panel, dy]
        scaled = product(split(total), upper, 1)
        ys[panel] = scaled
        yr[panel, here] = scaled
        shared = start([
            remote(
                ys.at[panel], yr.at[panel, here], ya_s.at[panel, i], ya_r.at[panel, i],
                device(o[0], 0, o[1], o[2]),
            )
            for i, o in enumerate(PEERS)
        ])
        for copy in shared:
            copy.wait_recv()
        whole = yr[panel].reshape(zf.shape[0], -1)
        zf[...] = zf[...] - product(split(whole), (vh[panel], vl[panel]), 0)
        pending += spread + across + shared

    result = []
    for o, (dx, dh) in enumerate(SLAB):
        there = slab_of(dx, dh)
        src = zf.at[pl.ds(pl.multiple_of(there * 32, 32), 32), :]
        dst = out.at[:, pl.ds(pl.multiple_of(mine * piece, piece), piece)]
        if o == 0:
            result.append(pltpu.make_async_copy(src, dst, own_sem.at[3]))
        else:
            result.append(remote(src, dst, zo_s.at[o], zo_r.at[o], device(dx, 0, dh, 0)))
    start(result)
    for copy in pending + [copy for sent in vectors_out for copy in sent[1:]]:
        copy.wait_send()
    for copy in result:
        copy.wait()


def per_device(eigvecs, row_map, reflectors, panel_factor, owners):
    total_rows = eigvecs.shape[1]
    local_rows = reflectors.shape[2]
    width = reflectors.shape[1]
    piece = total_rows // 64
    index = lax.slice(row_map, (0,), (total_rows,), (NB,)) // NB
    eig_tiles = eigvecs.reshape(4, total_rows // 128, 128).transpose(1, 0, 2)
    vectors = jnp.stack([lax.dynamic_index_in_dim(reflectors, owners[p], 0, False) for p in range(PANELS)])
    f32, bf16 = jnp.float32, jnp.bfloat16
    vmem, smem = pl.BlockSpec(memory_space=pltpu.VMEM), pl.BlockSpec(memory_space=pltpu.SMEM)
    half, all_width = 256, panel_factor.shape[1]
    dma = pltpu.SemaphoreType.DMA
    return pl.pallas_call(
        kernel,
        out_shape=jax.ShapeDtypeStruct((width, local_rows), f32),
        in_specs=[smem, smem, vmem, vmem, vmem],
        out_specs=vmem,
        scratch_shapes=[
            pltpu.VMEM((4, 16, 4, piece), f32),
            pltpu.VMEM((4, 16, 4, piece), f32),
            pltpu.VMEM((16, 4, 4, piece), f32),
            pltpu.VMEM((half, piece), f32),
            pltpu.VMEM((PANELS, 16, width, piece), f32),
            pltpu.VMEM((PANELS, all_width, piece), bf16),
            pltpu.VMEM((PANELS, all_width, piece), bf16),
            pltpu.VMEM((PANELS, 16, 16, all_width), f32),
            pltpu.VMEM((PANELS, 16, 16, all_width), f32),
            pltpu.VMEM((PANELS, 16, all_width), f32),
            pltpu.VMEM((PANELS, 4, 16, all_width), f32),
            pltpu.VMEM((PANELS, 16, all_width), f32),
            pltpu.VMEM((PANELS, 16, 16, all_width), f32),
            dma((4,)),
            dma((PANELS, 8)), dma((PANELS, 8)), dma((PANELS, 8)), dma((PANELS, 8)),
            dma((4,)), dma((4,)), dma((15,)), dma((15,)), dma((15,)), dma((15,)),
            dma((PANELS, 15)), dma((PANELS, 15)), dma((PANELS, 4)), dma((PANELS, 4)),
            dma((PANELS, 15)), dma((PANELS, 15)), dma((8,)), dma((8,)),
        ],
        compiler_params=pltpu.CompilerParams(
            collective_id=0, has_side_effects=True, vmem_limit_bytes=60 << 20
        ),
        name="back_transform",
    )(index // 2, index % 2, eig_tiles, vectors, panel_factor)


def solution(mesh):
    placed = (P(("col", "row"), None), P(), P(None, "col", "row"), P(), P())
    return jax.shard_map(
        per_device, mesh=mesh, in_specs=placed, out_specs=P("col", "row"), check_vma=False
    )
```

```python
import functools

import jax
import jax.numpy as jnp
from jax import lax
from jax.experimental import pallas as pl
from jax.experimental.pallas import tpu as pltpu
from jax.sharding import PartitionSpec as P

PANELS = 2
NB = 64
MESH = pl.DeviceIdType.MESH
PLANE = [(dx, dh, dl) for dx in range(4) for dh in range(2) for dl in range(2)]
PEERS = PLANE[1:]
SLAB = [(dx, dh) for dx in range(4) for dh in range(2)]


class Copies:
    def __init__(self):
        self.open = []

    def start(self, copies):
        for copy in copies:
            copy.start()
            self.open.append([copy, copy.is_remote])
        return copies

    def arrived(self, copy):
        for entry in self.open:
            if entry[0] is copy:
                if entry[1]:
                    copy.wait_recv()
                    entry[1] = False
                else:
                    copy.wait()
                    self.open = [other for other in self.open if other is not entry]
                return

    def finish(self):
        for copy, remote in self.open:
            if remote:
                copy.wait()
            elif copy.is_remote:
                copy.wait_send()
            else:
                copy.wait()
        self.open = []


def split(value):
    high = value.astype(jnp.bfloat16)
    return high, (value - high.astype(jnp.float32)).astype(jnp.bfloat16)


def product(left, right, contract):
    dims = (((1,), (contract,)), ((), ()))
    lh, ll = left
    rh, rl = right
    dot = functools.partial(lax.dot_general, dimension_numbers=dims, preferred_element_type=jnp.float32)
    return dot(lh, rh) + (dot(lh, rl) + dot(ll, rh))


def kernel(
    rows, eig, vin, factor, out,
    zg, za, zr, zf, vr, vh, vl, gh, gl, wp, wr, ws, wy, ys, yr,
    own_sem, va_s, va_r, vb_s, vb_r, za_s, za_r, zb_s, zb_r, zc_s, zc_r,
    ws_s, ws_r, wy_s, wy_r, ya_s, ya_r, zo_s, zo_r,
):
    row, col = lax.axis_index("row"), lax.axis_index("col")
    y, zl = lax.div(row, 2), lax.rem(row, 2)
    x, zh, core = lax.div(col, 4), lax.rem(lax.div(col, 2), 2), lax.rem(col, 2)

    def device(dx, dy, dh, dl, dc=0):
        there = (
            lax.rem(y + dy, 4) * 2 + lax.rem(zl + dl, 2),
            lax.rem(x + dx, 4) * 4 + lax.rem(zh + dh, 2) * 2 + lax.rem(core + dc, 2),
        )
        return there

    copies = Copies()
    start, arrived, finish = copies.start, copies.arrived, copies.finish

    def remote(src, dst, send, recv, there):
        return pltpu.make_async_remote_copy(
            src_ref=src, dst_ref=dst, send_sem=send, recv_sem=recv, device_id=there, device_id_type=MESH
        )

    def plane_of(dx, dh, dl):
        return lax.rem(x + dx, 4) * 4 + lax.rem(zh + dh, 2) * 2 + lax.rem(zl + dl, 2)

    def slab_of(dx, dh):
        return lax.rem(x + dx, 4) * 2 + lax.rem(zh + dh, 2)

    here, mine = plane_of(0, 0, 0), slab_of(0, 0)
    piece = zf.shape[1]

    barrier = pltpu.get_barrier_semaphore()
    for dx, dh, dl in PEERS:
        pl.semaphore_signal(barrier, inc=1, device_id=device(dx, 0, dh, dl), device_id_type=MESH)
    for dy in (1, 2, 3):
        pl.semaphore_signal(barrier, inc=1, device_id=device(0, dy, 0, 0), device_id_type=MESH)
    pl.semaphore_signal(barrier, inc=1, device_id=device(0, 0, 0, 0, 1), device_id_type=MESH)
    pl.semaphore_wait(barrier, len(PEERS) + 4)

    def vector_sends(panel):
        sends = []
        for o, (dx, dh) in enumerate(SLAB):
            there = slab_of(dx, dh)
            src = vin.at[panel, :, pl.ds(pl.multiple_of(there * piece, piece), piece)]
            if o == 0:
                sends.append(pltpu.make_async_copy(src, vr.at[panel, col], own_sem.at[panel]))
            else:
                sends.append(
                    remote(src, vr.at[panel, col], va_s.at[panel, o], va_r.at[panel, o], device(dx, 0, dh, 0))
                )
        return sends

    vectors_out = [start(vector_sends(0))]

    lane = lax.broadcasted_iota(jnp.int32, (4, 128), 1)

    def gather(dy, target):
        yy = lax.rem(y + dy, 4)

        def body(step, carry):
            xz, low = lax.div(step, 2), lax.rem(step, 2)
            first = (yy * 2 + low) * (8 * piece // NB) + xz * (piece // NB)
            for tile in range(piece // 128):
                one, two = first + 2 * tile, first + 2 * tile + 1
                a, b = eig[rows[one] >> 7], eig[rows[two] >> 7]
                a_odd, b_odd = jnp.full((4, 128), rows[one] & NB), jnp.full((4, 128), rows[two] & NB)
                a = jnp.where(a_odd == 0, a, pltpu.roll(a, 64, 1))
                b = jnp.where(b_odd != 0, b, pltpu.roll(b, 64, 1))
                target[step, :, tile * 128 : (tile + 1) * 128] = jnp.where(lane < 64, a, b)
            return carry

        lax.fori_loop(0, 16, body, 0)

    along_y = []
    for dy in (2, 1, 3):
        gather(dy, zg.at[dy])
        along_y.append(remote(zg.at[dy], za.at[dy], za_s.at[dy], za_r.at[dy], device(0, dy, 0, 0)))
        start(along_y[-1:])
    gather(0, za.at[0])
    near = [
        remote(za.at[0, plane_of(*o)], zr.at[here, 0], zb_s.at[i], zb_r.at[i], device(o[0], 0, o[1], o[2]))
        for i, o in enumerate(PEERS)
    ]
    start(near)
    for copy in along_y:
        arrived(copy)
    far = [
        remote(
            za.at[pl.ds(1, 3), plane_of(*o)], zr.at[here, pl.ds(1, 3)], zc_s.at[i], zc_r.at[i],
            device(o[0], 0, o[1], o[2]),
        )
        for i, o in enumerate(PEERS)
    ]
    start(far)
    own = pltpu.make_async_copy(za.at[:, here], zr.at[here], own_sem.at[2])
    start([own])

    def exchange(panel):
        passed = []
        for o, (dx, dh) in enumerate(SLAB):
            source = lax.rem(x + 4 - dx, 4) * 4 + lax.rem(zh + dh, 2) * 2 + core
            arrived(vectors_out[panel][o])
            passed += start([
                remote(
                    vr.at[panel, source], vr.at[panel, source], vb_s.at[panel, o], vb_r.at[panel, o],
                    device(0, 0, 0, 0, 1),
                )
            ])
        return passed

    def split_vectors(panel, passed):
        for copy in passed:
            arrived(copy)

        def body(step, carry):
            high, low = split(vr[panel, step])
            vh[panel, pl.ds(pl.multiple_of(step * 32, 32), 32), :] = high
            vl[panel, pl.ds(pl.multiple_of(step * 32, 32), 32), :] = low
            return carry

        lax.fori_loop(0, 16, body, 0)

    split_vectors(0, exchange(0))
    for copy in near + far + [own]:
        arrived(copy)

    def assemble(step, carry):
        chip, dy = lax.div(step, 4), lax.rem(step, 4)
        rows = jnp.concatenate([zr[2 * chip, dy], zr[2 * chip + 1, dy]], axis=0)
        place = chip * 32 + lax.rem(y + 4 - dy, 4) * 8
        zf[pl.ds(pl.multiple_of(place, 8), 8), :] = rows
        return carry

    lax.fori_loop(0, 32, assemble, 0)

    def blocks(value):
        return value.reshape(16, 16, value.shape[-1])

    wp[0] = blocks(product(split(zf[...]), (vh[0], vl[0]), 1))
    for panel in range(PANELS):
        spread = start([
            remote(
                wp.at[panel, plane_of(*o)], wr.at[panel, here], ws_s.at[panel, i], ws_r.at[panel, i],
                device(o[0], 0, o[1], o[2]),
            )
            for i, o in enumerate(PEERS)
        ])
        if panel == 0:
            vectors_out.append(start(vector_sends(1)))
        else:
            zf[...] = zf[...] - product(split(yr[0].reshape(zf.shape[0], -1)), (vh[0], vl[0]), 0)
        row_i = lax.broadcasted_iota(jnp.int32, factor.shape[1:], 0)
        col_i = lax.broadcasted_iota(jnp.int32, factor.shape[1:], 1)
        upper = split(jnp.where(row_i <= col_i, factor[panel], 0.0))
        total = wp[panel, here]
        for (dx, dh, dl), copy in zip(PEERS, spread):
            arrived(copy)
            total = total + wr[panel, lax.rem(x + 4 - dx, 4) * 4 + lax.rem(zh + dh, 2) * 2 + lax.rem(zl + dl, 2)]
        ws[panel] = total
        across = start([
            remote(ws.at[panel], wy.at[panel, dy], wy_s.at[panel, dy], wy_r.at[panel, dy], device(0, dy, 0, 0))
            for dy in (1, 2, 3)
        ])
        for dy, copy in zip((1, 2, 3), across):
            arrived(copy)
            total = total + wy[panel, dy]
        scaled = product(split(total), upper, 1)
        ys[panel] = scaled
        yr[panel, here] = scaled
        shared = start([
            remote(
                ys.at[panel], yr.at[panel, here], ya_s.at[panel, i], ya_r.at[panel, i],
                device(o[0], 0, o[1], o[2]),
            )
            for i, o in enumerate(PEERS)
        ])
        if panel == 0:
            split_vectors(1, exchange(1))
            wp[1] = blocks(product(split(zf[...]), (vh[1], vl[1]), 1))
            gh[...], gl[...] = split(product((vh[0], vl[0]), (vh[1], vl[1]), 1))
        for copy in shared:
            arrived(copy)
        whole = split(yr[panel].reshape(zf.shape[0], -1))
        if panel == 0:
            wp[1] = wp[1] - blocks(product(whole, (gh[...], gl[...]), 0))
        else:
            zf[...] = zf[...] - product(whole, (vh[1], vl[1]), 0)

    result = []
    for o, (dx, dh) in enumerate(SLAB):
        there = slab_of(dx, dh)
        src = zf.at[pl.ds(pl.multiple_of(there * 32, 32), 32), :]
        dst = out.at[:, pl.ds(pl.multiple_of(mine * piece, piece), piece)]
        if o == 0:
            result.append(pltpu.make_async_copy(src, dst, own_sem.at[3]))
        else:
            result.append(remote(src, dst, zo_s.at[o], zo_r.at[o], device(dx, 0, dh, 0)))
    start(result)
    finish()


def fetch_kernel(owners, slots, out, sem):
    copies = [pltpu.make_async_copy(slots.at[owners[p]], out.at[p], sem.at[p]) for p in range(PANELS)]
    for copy in copies:
        copy.start()
    for copy in copies:
        copy.wait()


def per_device(eigvecs, row_map, reflectors, panel_factor, owners):
    total_rows = eigvecs.shape[1]
    local_rows = reflectors.shape[2]
    width = reflectors.shape[1]
    piece = total_rows // 64
    starts = lax.slice(row_map, (0,), (total_rows,), (NB,))
    eig_tiles = eigvecs.reshape(4, total_rows // 128, 128).transpose(1, 0, 2)
    f32, bf16 = jnp.float32, jnp.bfloat16
    vmem, smem = pl.BlockSpec(memory_space=pltpu.VMEM), pl.BlockSpec(memory_space=pltpu.SMEM)
    half, all_width = 256, panel_factor.shape[1]
    dma = pltpu.SemaphoreType.DMA
    vectors = pl.pallas_call(
        fetch_kernel,
        out_shape=jax.ShapeDtypeStruct((PANELS, width, local_rows), f32),
        in_specs=[smem, pl.BlockSpec(memory_space=pltpu.HBM)],
        out_specs=vmem,
        scratch_shapes=[dma((PANELS,))],
        compiler_params=pltpu.CompilerParams(vmem_limit_bytes=8 << 20),
        name="fetch_slots",
    )(owners, reflectors)
    return pl.pallas_call(
        kernel,
        out_shape=jax.ShapeDtypeStruct((width, local_rows), f32),
        in_specs=[smem, vmem, vmem, vmem],
        out_specs=vmem,
        scratch_shapes=[
            pltpu.VMEM((4, 16, 4, piece), f32),
            pltpu.VMEM((4, 16, 4, piece), f32),
            pltpu.VMEM((16, 4, 4, piece), f32),
            pltpu.VMEM((half, piece), f32),
            pltpu.VMEM((PANELS, 16, width, piece), f32),
            pltpu.VMEM((PANELS, all_width, piece), bf16),
            pltpu.VMEM((PANELS, all_width, piece), bf16),
            pltpu.VMEM((all_width, all_width), bf16),
            pltpu.VMEM((all_width, all_width), bf16),
            pltpu.VMEM((PANELS, 16, 16, all_width), f32),
            pltpu.VMEM((PANELS, 16, 16, all_width), f32),
            pltpu.VMEM((PANELS, 16, all_width), f32),
            pltpu.VMEM((PANELS, 4, 16, all_width), f32),
            pltpu.VMEM((PANELS, 16, all_width), f32),
            pltpu.VMEM((PANELS, 16, 16, all_width), f32),
            dma((4,)),
            dma((PANELS, 8)), dma((PANELS, 8)), dma((PANELS, 8)), dma((PANELS, 8)),
            dma((4,)), dma((4,)), dma((15,)), dma((15,)), dma((15,)), dma((15,)),
            dma((PANELS, 15)), dma((PANELS, 15)), dma((PANELS, 4)), dma((PANELS, 4)),
            dma((PANELS, 15)), dma((PANELS, 15)), dma((8,)), dma((8,)),
        ],
        compiler_params=pltpu.CompilerParams(
            collective_id=0, has_side_effects=True, vmem_limit_bytes=40 << 20
        ),
        name="back_transform",
    )(starts, eig_tiles, vectors, panel_factor)


def solution(mesh):
    placed = (P(("col", "row"), None), P(), P(None, "col", "row"), P(), P())
    return jax.shard_map(
        per_device, mesh=mesh, in_specs=placed, out_specs=P("col", "row"), check_vma=False
    )
```
